32 devices in a mesh: row: 8 (over z, y), col: 4 (over x, core).
Axes of the slice: x: 2, y: 2, z: 4, core: 2. Of those that a mesh axis runs over, the one named last changes fastest.
Arguments:
- relation: float32 [16384, 16384], P('row', 'col'), as said below
- dosage: int32 [512, 16384], P(None, 'col'), may hold values from 0 to 200
- freq: int32 [512], replicated, may hold values from 500 to 9500
- panel: int32 [1], replicated, may hold values from 0 to 502
Outputs:
- reduced: float32 [16384, 16384], P('row', 'col')
The draws below stay inside these ranges and needn't reach their ends.
Inputs may be any that keep to these rules, and one draw needn't show every extreme that they name: relation is symmetric.
All inputs are finite; a program needn't handle non-finite values.
Results may differ from the reference program's by a relative error of at most 0.00045.
Values may be sent and summed in bfloat16 or wider, within the bound.
No kernel may reach another device: no remote copies, remote signals or barrier semaphores. Data moves between devices by JAX's collectives and lax.ppermute only.
A program may use at most 192 MiB of HBM per device.

```python
import jax
import jax.numpy as jnp
from jax import lax

N = 16384
B = 32
M = 512


def draw_relation(key, part):
    first_key, second_key = jax.random.split(key)
    noise_draw = jax.random.normal(first_key, (N, N), jnp.float32)
    row_ids = jnp.arange(N, dtype=jnp.int32)[:, None]
    col_ids = jnp.arange(N, dtype=jnp.int32)[None, :]
    diagonal = 1.0 + 0.5 * jax.random.uniform(second_key, (N,), jnp.float32)
    symmetric = 0.035 * (noise_draw + noise_draw.T)
    kinship = jnp.where(jnp.abs(row_ids - col_ids) == B, 0.4, 0.0)
    return symmetric + kinship + jnp.where(row_ids == col_ids, diagonal[None, :], 0.0)


def touch_ends(drawn, own_key, smallest, largest):
    longest = drawn.shape.index(max(drawn.shape))
    spots = []
    for shift in (0, 1):
        where = [jax.random.randint(jax.random.fold_in(own_key, axis), (), 0, length) for axis, length in enumerate(drawn.shape)]
        where[longest] = (where[longest] + shift) % drawn.shape[longest]
        spots.append(tuple(where))
    return drawn.at[spots[0]].set(smallest).at[spots[1]].set(largest)


def setup_inputs(seed: int = 0) -> dict:
    splits = jax.random.split(jax.random.key(seed), 5)
    return {
        "relation": draw_relation(jax.random.fold_in(splits[4], 71), 0),
        "dosage": touch_ends(jax.random.randint(splits[1], (M, N), 0, 201), jax.random.fold_in(splits[1], 1), 0, 200).astype(jnp.int32),
        "freq": touch_ends(jax.random.randint(splits[2], (M,), 500, 9501), jax.random.fold_in(splits[2], 1), 500, 9500).astype(jnp.int32),
        "panel": jax.random.randint(splits[3], (1,), 0, N // B - 9).astype(jnp.int32),
    }


HIGH = lax.Precision.HIGHEST

def standardize(dosage, freq):
    allele = freq.astype(jnp.float32) / 10000.0
    spread = jnp.sqrt(2.0 * allele * (1.0 - allele))
    scaled = (dosage.astype(jnp.float32) / 100.0 - 2.0 * allele[:, None]) / spread[:, None]
    return scaled.astype(jnp.bfloat16)

def householder(panel_block, first_row):
    height = panel_block.shape[0]
    breadth = panel_block.shape[1]
    row_ids = jnp.arange(height, dtype=jnp.int32)
    slots = jnp.arange(breadth, dtype=jnp.int32)

    def reflect_step(column_id, carry):
        panel_work, vectors, triangle = carry
        pivot = first_row + column_id
        column = lax.optimization_barrier(jnp.sum(jnp.where(slots[None, :] == column_id, panel_work, 0.0), axis=1))
        below = jnp.where(row_ids >= pivot, column, 0.0)
        at_pivot = row_ids == pivot
        alpha = jnp.sum(jnp.where(at_pivot, column, 0.0))
        length = jnp.sqrt(jnp.sum(below * below))
        signum = jnp.where(alpha >= 0.0, 1.0, -1.0)
        vector = below + jnp.where(at_pivot, signum * length, 0.0)
        scale_tau = 2.0 / jnp.sum(vector * vector)
        project = jnp.dot(vector, panel_work, precision=HIGH)
        panel_work = panel_work - scale_tau * vector[:, None] * project[None, :]
        cross = jnp.dot(vector, vectors, precision=HIGH)
        new_column = -scale_tau * jnp.dot(triangle, cross, precision=HIGH)
        picked = jnp.where(slots == column_id, 1.0, 0.0).astype(panel_work.dtype)
        triangle = triangle + new_column[:, None] * picked[None, :] + scale_tau * picked[:, None] * picked[None, :]
        vectors = vectors + vector[:, None] * picked[None, :]
        return (panel_work, vectors, triangle)
    start = (panel_block, jnp.zeros_like(panel_block), jnp.zeros((breadth, breadth), panel_block.dtype))
    return lax.fori_loop(0, breadth, reflect_step, start)

def reference(relation, dosage, freq, panel):
    scaled = standardize(dosage, freq)
    grown = relation + jnp.dot(scaled.T, scaled, preferred_element_type=jnp.float32) / M
    panel_index = panel[0].astype(jnp.int32)
    block = lax.dynamic_slice_in_dim(grown, (panel_index * B).astype(jnp.int32), B, 1)
    panel_work, vectors, triangle = householder(block, (panel_index + 1) * B)
    applied = jnp.dot(jnp.dot(grown, vectors, precision=HIGH), triangle, precision=HIGH)
    middle = jnp.dot(triangle.T, jnp.dot(vectors.T, applied, precision=HIGH), precision=HIGH)
    adjusted = applied - 0.5 * jnp.dot(vectors, middle, precision=HIGH)
    left_side = jnp.concatenate([vectors, adjusted], axis=1)
    right_side = jnp.concatenate([adjusted, vectors], axis=1)
    return grown - jnp.dot(left_side, right_side.T, precision=HIGH)
```

```python
import functools

import jax
import jax.numpy as jnp
from jax import lax
from jax.experimental import pallas as pl
from jax.experimental.pallas import tpu as pltpu
from jax.sharding import PartitionSpec as P

B = 32
M = 512
F32 = jnp.float32
BF16 = jnp.bfloat16
HIGH = lax.Precision.HIGHEST
NN = (((1,), (0,)), ((), ()))
NT = (((1,), (1,)), ((), ()))
TN = (((0,), (0,)), ((), ()))


def split(value):
    high = value.astype(BF16)
    return high, (value - high.astype(F32)).astype(BF16)


def split_3(value):
    high = value.astype(BF16)
    rest = value - high.astype(F32)
    middle = rest.astype(BF16)
    return high, middle, (rest - middle.astype(F32)).astype(BF16)


def dot_3(a, b):
    ah, am, al = split_3(a)
    bh, bm, bl = split_3(b)
    return lax.dot_general(
        jnp.concatenate([ah, ah, am, ah, am, al], axis=0),
        jnp.concatenate([bh, bm, bh, bl, bm, bh], axis=0),
        TN,
        preferred_element_type=F32,
    )


def fold(value, count):
    total = value[:B]
    for k in range(1, count):
        total = total + value[k * B : (k + 1) * B]
    return total


ROOM = 30 * 2**20


def room(**more):
    return pltpu.CompilerParams(vmem_limit_bytes=ROOM, **more)


def whole(shape):
    return pl.BlockSpec(shape, lambda i, *place: (0,) * len(shape))


def standardize(dosage, freq, individuals=1):
    allele = freq.astype(F32) / 10000.0
    spread = jnp.sqrt(2.0 * allele * (1.0 - allele))
    allele, spread = (jnp.expand_dims(value, individuals) for value in (allele, spread))
    scaled = (dosage.astype(F32) / 100.0 - 2.0 * allele) / spread
    return scaled.astype(BF16)


def strip_kernel(place_ref, source_ref, strip_ref, turned_ref):
    turned_ref[...] = source_ref[...].astype(F32).T
    strip_ref[...] = turned_ref[pl.ds(pl.multiple_of(place_ref[1], B), B), :]


def take_strip(source, offset):
    rows = source.shape[0]
    width = min(128, source.shape[1])
    place = jnp.stack([offset // width, offset % width]).astype(jnp.int32)
    return pl.pallas_call(
        strip_kernel,
        out_shape=jax.ShapeDtypeStruct((B, rows), F32),
        grid_spec=pltpu.PrefetchScalarGridSpec(
            num_scalar_prefetch=1,
            grid=(1,),
            in_specs=[pl.BlockSpec((rows, width), lambda i, place: (0, place[0]))],
            out_specs=pl.BlockSpec((B, rows), lambda i, place: (0, 0)),
            scratch_shapes=[pltpu.VMEM((width, rows), F32)],
        ),
        compiler_params=room(),
        name="strip",
    )(place, source)


def lifted(strip, ids, factor, lift):
    slots = lax.broadcasted_iota(jnp.int32, (B, 1), 0)
    select = jnp.where(ids == slots, 1.0, 0.0).astype(BF16)
    taken = lax.dot_general(
        jnp.concatenate(split_3(factor), axis=0),
        jnp.concatenate([select] * 3, axis=0),
        TN,
        preferred_element_type=F32,
    )
    return dot_3(lift, jnp.where(ids >= 0, strip, 0.0) - taken)


def lane_ids(width, start):
    return start + lax.broadcasted_iota(jnp.int32, (1, width), 1)


def panel_kernel(place_ref, raw_ref, chosen_ref, scaled_ref, strip_ref, small_ref):
    strip = raw_ref[...] + jnp.dot(
        chosen_ref[...], scaled_ref[...], preferred_element_type=F32
    ) * (1.0 / M)
    strip_ref[...] = strip
    ids = lane_ids(strip.shape[1], place_ref[0])
    slots = lax.broadcasted_iota(jnp.int32, (B, 1), 0)
    select = jnp.where(ids == slots, 1.0, 0.0).astype(BF16)
    parts = jnp.concatenate(split_3(strip), axis=0)
    rest = jnp.where(ids >= B, parts, jnp.zeros_like(parts))
    square = lax.dot_general(
        jnp.concatenate([select, rest], axis=0), parts, NT, preferred_element_type=F32
    )
    square = square[:, :B] + square[:, B : 2 * B] + square[:, 2 * B :]
    small_ref[:B, :] = square[:B]
    small_ref[B:, :] = fold(square[B:], 3)


def panel_block(place, raw, chosen, scaled):
    width = raw.shape[1]
    return pl.pallas_call(
        panel_kernel,
        out_shape=(
            jax.ShapeDtypeStruct((B, width), F32),
            jax.ShapeDtypeStruct((2 * B, B), F32),
        ),
        grid_spec=pltpu.PrefetchScalarGridSpec(
            num_scalar_prefetch=1,
            grid=(1,),
            in_specs=[whole(raw.shape), whole(chosen.shape), whole(scaled.shape)],
            out_specs=(whole((B, width)), whole((2 * B, B))),
        ),
        compiler_params=room(),
        name="panel",
    )(place, raw, chosen, scaled)


def product_kernel(
    place_ref, strip_ref, factor_ref, lift_ref, scaled_ref, relation_ref,
    vecs_ref, sums_ref, marks_ref, columns_ref,
):
    @pl.when(pl.program_id(0) == 0)
    def _():
        width = strip_ref.shape[1]
        ids = lane_ids(width, place_ref[0])
        vecs = lifted(strip_ref[...], ids, factor_ref[...], lift_ref[...])
        vecs_ref[...] = vecs
        high, low = split(vecs)
        both = jnp.concatenate([high, low], axis=0)
        both = jnp.concatenate([both, jnp.zeros_like(both)], axis=0)
        columns_ref[...] = both.astype(F32).T.astype(BF16)
        marks_ref[...] = fold(
            lax.dot_general(both, scaled_ref[...], NT, preferred_element_type=F32), 2
        )

    step = sums_ref.shape[1]
    here = pl.ds(pl.multiple_of(pl.program_id(0) * step, step), step)
    high, low = split(relation_ref[here, :])
    columns = columns_ref[...]
    product = jnp.dot(high, columns, preferred_element_type=F32) + jnp.dot(
        low, columns, preferred_element_type=F32
    )
    sums_ref[...] = fold(product.T, 2)


def tile_product(place, strip, factor, lift, scaled, relation):
    rows, width = relation.shape
    step = min(256, rows)
    return pl.pallas_call(
        product_kernel,
        out_shape=(
            jax.ShapeDtypeStruct((B, width), F32),
            jax.ShapeDtypeStruct((B, rows), F32),
            jax.ShapeDtypeStruct((B, M), F32),
        ),
        grid_spec=pltpu.PrefetchScalarGridSpec(
            num_scalar_prefetch=1,
            grid=(rows // step,),
            in_specs=[
                whole(strip.shape),
                whole((B, B)),
                whole((B, B)),
                whole(scaled.shape),
                pl.BlockSpec(memory_space=pltpu.VMEM),
            ],
            out_specs=(
                whole((B, width)),
                pl.BlockSpec((B, step), lambda i, place: (0, i)),
                whole((B, M)),
            ),
            scratch_shapes=[pltpu.VMEM((width, 4 * B), BF16)],
        ),
        cost_estimate=pl.CostEstimate(
            flops=16 * B * rows * width, bytes_accessed=4 * rows * width, transcendentals=0
        ),
        compiler_params=room(),
        name="product",
    )(place, strip, factor, lift, scaled, relation)


def rows_kernel(
    place_ref, raw_ref, chosen_ref, scaled_ref, factor_ref, lift_ref, sums_ref,
    vecs_ref, inner_ref, turned_ref,
):
    scaled = scaled_ref[...]
    strip = raw_ref[...] + jnp.dot(
        chosen_ref[...], scaled, preferred_element_type=F32
    ) * (1.0 / M)
    ids = lane_ids(strip.shape[1], place_ref[0])
    vecs = lifted(strip, ids, factor_ref[...], lift_ref[...])
    vecs_ref[...] = vecs
    square = lax.dot_general(
        jnp.concatenate(split(vecs), axis=0),
        jnp.concatenate(split(sums_ref[...]), axis=0),
        NT,
        preferred_element_type=F32,
    )
    inner_ref[...] = fold(square[:, :B] + square[:, B:], 2)
    turned_ref[...] = (scaled.astype(F32) * (1.0 / M)).T.astype(BF16)


def row_block(place, raw, chosen, scaled, factor, lift, sums):
    args = (raw, chosen, scaled, factor, lift, sums)
    outs = ((raw.shape, F32), ((B, B), F32), (scaled.shape[::-1], BF16))
    return pl.pallas_call(
        rows_kernel,
        out_shape=tuple(jax.ShapeDtypeStruct(*out) for out in outs),
        grid_spec=pltpu.PrefetchScalarGridSpec(
            num_scalar_prefetch=1,
            grid=(1,),
            in_specs=[whole(a.shape) for a in args],
            out_specs=tuple(whole(out[0]) for out in outs),
        ),
        compiler_params=room(),
        name="rows",
    )(place, *args)


def reflect_kernel(small_ref, factor_ref, lift_ref, triangle_ref):
    rows = lax.broadcasted_iota(jnp.int32, (B, B), 0)
    lanes = lax.broadcasted_iota(jnp.int32, (B, B), 1)
    row = lax.broadcasted_iota(jnp.int32, (B, 1), 0)
    lane = lax.broadcasted_iota(jnp.int32, (1, B), 1)
    eye = jnp.where(rows == lanes, 1.0, 0.0).astype(F32)
    work = small_ref[:B, :]
    cross = small_ref[B:, :]
    lift = eye
    triangle = jnp.zeros((B, B), F32)
    diagonal = jnp.zeros((1, B), F32)
    for j in range(B):
        column = jnp.where(row >= j, work[:, j : j + 1], 0.0)
        lift_column = lift[:, j : j + 1]
        cross_column = cross[:, j : j + 1]
        inner = jnp.sum(column * work, axis=0, keepdims=True) + jnp.sum(
            lift_column * cross, axis=0, keepdims=True
        )
        square = inner[:, j : j + 1]
        alpha = work[j : j + 1, j : j + 1]
        length = jnp.sqrt(square)
        shift = jnp.where(alpha >= 0.0, length, -length)
        tau = 1.0 / (length * (length + jnp.abs(alpha)))
        inner = inner + shift * work[j : j + 1, :]
        vector = column + jnp.where(row == j, shift, 0.0)
        kappa = jnp.where(lane > j, tau * inner, 0.0)
        work = work - vector * kappa
        work = work + jnp.where((rows == j) & (lanes == j), shift, 0.0)
        lift = lift - lift_column * kappa
        cross = cross - cross_column * kappa
        past = jnp.sum(triangle * jnp.where(lane < j, inner, 0.0), axis=1, keepdims=True)
        new = tau * (jnp.where(row == j, 1.0, 0.0) - past)
        triangle = jnp.where(lanes == j, new, triangle)
        diagonal = jnp.where(lane == j, -shift, diagonal)
    factor_ref[...] = jnp.where(rows < lanes, work, 0.0) + jnp.where(rows == lanes, diagonal, 0.0)
    lift_ref[...] = lift
    triangle_ref[...] = triangle


def reflect(small):
    out = jax.ShapeDtypeStruct((B, B), F32)
    return pl.pallas_call(
        reflect_kernel, out_shape=(out,) * 3, compiler_params=room(), name="reflect"
    )(small)


def update_kernel(
    triangle_ref, inner_ref, marks_ref, turned_ref, scaled_rows_ref, vecs_rows_ref,
    sums_rows_ref, scaled_cols_ref, vecs_cols_ref, sums_cols_ref, relation_ref,
    out_ref, left_ref, half_ref,
):
    def dot(a, b, dims):
        return lax.dot_general(a, b, dims, precision=HIGH, preferred_element_type=F32)

    def parts(vecs, sums, scaled):
        marks = jnp.concatenate(split(marks_ref[...] * (1.0 / M)), axis=0)
        full = sums + fold(
            lax.dot_general(marks, scaled, NN, preferred_element_type=F32), 2
        )
        th, tl = split(triangle_ref[...])
        hh, hl = split(-half_ref[...])
        fh, fl = split(full)
        vh, vl = split(vecs)
        adjusted = lax.dot_general(
            jnp.concatenate([th, th, tl, hh, hh, hl], axis=0),
            jnp.concatenate([fh, fl, fh, vh, vl, vh], axis=0),
            TN,
            preferred_element_type=F32,
        )
        return (vh, vl) + split(adjusted)

    @pl.when(pl.program_id(0) == 0)
    def _():
        triangle = triangle_ref[...]
        marks = marks_ref[...]
        inner = inner_ref[...] + dot(marks, marks, NT) * (1.0 / M)
        half_ref[...] = 0.5 * dot(triangle, dot(inner, triangle, NN), TN)
        vh, vl, ah, al = parts(
            vecs_rows_ref[...], sums_rows_ref[...], scaled_rows_ref[...]
        )
        left = jnp.concatenate([vh, vh, vl, vl, ah, ah, al, al], axis=0)
        left_ref[...] = left.astype(F32).T.astype(BF16)

    scaled = scaled_cols_ref[...]
    vh, vl, ah, al = parts(vecs_cols_ref[...], sums_cols_ref[...], scaled)
    right = -jnp.concatenate([ah, al, ah, al, vh, vl, vh, vl], axis=0)
    rows, step = out_ref.shape
    here = pl.ds(pl.multiple_of(pl.program_id(0) * step, step), step)
    chunk = min(512, rows)
    for k in range(rows // chunk):
        some = pl.ds(k * chunk, chunk)
        out_ref[some, :] = (
            relation_ref[some, here]
            + jnp.dot(turned_ref[some, :], scaled, preferred_element_type=F32)
            + jnp.dot(left_ref[some, :], right, preferred_element_type=F32)
        )


def tile_update(triangle, inner, marks, of_rows, of_cols, relation):
    rows, width = relation.shape
    step = min(512, width)

    def full(value):
        return pl.BlockSpec(value.shape, lambda i: (0, 0), pipeline_mode=pl.Buffered(1))

    def slab(value):
        return pl.BlockSpec((value.shape[0], step), lambda i: (0, i))

    fixed = (triangle, inner, marks) + of_rows
    return pl.pallas_call(
        update_kernel,
        out_shape=jax.ShapeDtypeStruct((rows, width), F32),
        grid=(width // step,),
        in_specs=[full(value) for value in fixed]
        + [slab(value) for value in of_cols]
        + [pl.BlockSpec(memory_space=pltpu.VMEM)],
        out_specs=slab(relation),
        scratch_shapes=[pltpu.VMEM((rows, 8 * B), BF16), pltpu.VMEM((B, B), F32)],
        cost_estimate=pl.CostEstimate(
            flops=2 * (M + 8 * B) * rows * width,
            bytes_accessed=8 * rows * width,
            transcendentals=0,
        ),
        compiler_params=room(),
        name="update",
    )(*fixed, *of_cols, relation)


def swap(value, axis, size, bit):
    return lax.ppermute(value, axis, [(i, i ^ bit) for i in range(size)])


def bits_of(size):
    return [1 << b for b in range(size.bit_length() - 1)]


def make_body(n_row, n_col):
    per = n_row // n_col
    both = ("row", "col")

    def body(relation, dosage, freq, panel):
        tile_rows, tile_cols = relation.shape
        row_id = lax.axis_index("row")
        col_id = lax.axis_index("col")
        place = panel[0]
        first_row = (place + 1) * B
        panel_col = place * B // tile_cols
        panel_off = place * B % tile_cols
        own_col = row_id // per

        def from_panel(value, bits):
            for bit in bits:
                other = swap(value, "col", n_col, bit)
                value = jnp.where(((col_id ^ panel_col) & bit) != 0, other, value)
            return value

        def to_column(block):
            total = jnp.where(own_col == col_id, block, 0.0)
            received = []
            for shift in range(1, n_col):
                pairs = []
                for c in range(n_col):
                    for s in range(per):
                        source = (c * per + s) * n_col + c
                        target = (((c + shift) % n_col) * per + s) * n_col + c
                        pairs.append((source, target))
                received.append(lax.ppermute(block, both, pairs))
            for other in received:
                total = total + other
            return total

        def join_column(block):
            mine = row_id % per
            parts = [None] * per
            got = [block]
            for shift in range(1, per):
                pairs = [
                    (r, (r // per) * per + (r % per) ^ shift) for r in range(n_row)
                ]
                got.append(lax.ppermute(block, "row", pairs))
            for s in range(per):
                value = got[0]
                for shift in range(1, per):
                    value = jnp.where((mine ^ s) == shift, got[shift], value)
                parts[s] = value
            return jnp.concatenate(parts, axis=1)

        raw_rows = take_strip(relation, panel_off)
        held = pltpu.with_memory_space_constraint(relation, pltpu.VMEM)
        raw_rows = from_panel(raw_rows, [1])
        dosage, raw_rows = lax.optimization_barrier((dosage, raw_rows))
        scaled = standardize(dosage, freq)
        chosen = take_strip(dosage, panel_off)
        chosen = from_panel(standardize(chosen, freq, 0), bits_of(n_col))
        raw_rows = from_panel(raw_rows, bits_of(n_col)[1:])

        own = lax.dynamic_slice_in_dim(scaled, (row_id % per) * tile_rows, tile_rows, 1)

        def spread_rows(value, bit):
            pairs = []
            for r in range(n_row):
                for c in range(n_col):
                    apart = c ^ (r // per)
                    if bit == 1:
                        if apart == 0:
                            pairs.append((r * n_col + c, r * n_col + (c ^ 1)))
                    elif (apart & ~1) & ~(bit - 1) == 0:
                        pairs.append((r * n_col + c, r * n_col + (c ^ bit)))
            other = lax.ppermute(value, both, pairs)
            apart = col_id ^ own_col
            if bit == 1:
                take = (apart & 1) != 0
            else:
                take = (apart & bit) != 0
            return jnp.where(take, other, value)

        own = spread_rows(own, 1)
        core = col_id % 2
        half = M // 2
        part = lax.dynamic_slice_in_dim(own, core * half, half, 0)
        part, raw_rows = lax.optimization_barrier((part, raw_rows))
        for bit in bits_of(n_col)[1:]:
            part = spread_rows(part, bit)
        other = swap(part, "col", n_col, 1)
        rows_scaled = jnp.concatenate(
            [jnp.where(core == 0, part, other), jnp.where(core == 0, other, part)], axis=0
        )

        raw_cols = join_column(to_column(raw_rows))
        place_cols = jnp.reshape(col_id * tile_cols - first_row, (1,)).astype(jnp.int32)
        place_rows = jnp.reshape(row_id * tile_rows - first_row, (1,)).astype(jnp.int32)
        strip_cols, small = panel_block(place_cols, raw_cols, chosen, scaled)
        for bit in bits_of(n_col):
            small = small + swap(small, "col", n_col, bit)
        small, rows_scaled = lax.optimization_barrier((small, rows_scaled))
        factor, lift, triangle = reflect(small)

        vecs_cols, part_sums, part_marks = tile_product(
            place_cols, strip_cols, factor, lift, scaled, held
        )
        sums = jnp.concatenate([part_sums, part_marks], axis=1)
        width = sums.shape[1] // 2
        kept = lax.dynamic_slice_in_dim(sums, core * width, width, 1)
        sent = lax.dynamic_slice_in_dim(sums, (1 - core) * width, width, 1)
        vecs_rows, inner, turned = row_block(
            place_rows, raw_rows, chosen, rows_scaled, factor, lift, part_sums
        )
        kept = kept + swap(sent, "col", n_col, 1)
        inner = inner + swap(inner, "col", n_col, 1)
        for bit in bits_of(n_col)[1:]:
            other = swap(kept, "col", n_col, bit)
            other, inner = lax.optimization_barrier((other, inner))
            kept = kept + other
            inner = inner + swap(inner, "col", n_col, bit)
        other = swap(kept, "col", n_col, 1)
        sums = jnp.concatenate(
            [jnp.where(core == 0, kept, other), jnp.where(core == 0, other, kept)], axis=1
        )
        sums_rows, marks = sums[:, :tile_rows], sums[:, tile_rows:]
        for bit in bits_of(n_row):
            inner = inner + swap(inner, "row", n_row, bit)
        sums_cols = join_column(to_column(sums_rows))
        return tile_update(
            triangle,
            inner,
            marks,
            (turned, rows_scaled, vecs_rows, sums_rows),
            (scaled, vecs_cols, sums_cols),
            held,
        )

    return body


def solution(mesh):
    placed = (P("row", "col"), P(None, "col"), P(), P())
    body = make_body(mesh.shape["row"], mesh.shape["col"])
    return jax.shard_map(
        body, mesh=mesh, in_specs=placed, out_specs=P("row", "col"), check_vma=False
    )
```

```python
import functools

import jax
import jax.numpy as jnp
from jax import lax
from jax.experimental import pallas as pl
from jax.experimental.pallas import tpu as pltpu
from jax.sharding import PartitionSpec as P

B = 32
M = 512
F32 = jnp.float32
BF16 = jnp.bfloat16
HIGH = lax.Precision.HIGHEST
NN = (((1,), (0,)), ((), ()))
NT = (((1,), (1,)), ((), ()))
TN = (((0,), (0,)), ((), ()))


def split(value):
    high = value.astype(BF16)
    return high, (value - high.astype(F32)).astype(BF16)


def split_3(value):
    high = value.astype(BF16)
    rest = value - high.astype(F32)
    middle = rest.astype(BF16)
    return high, middle, (rest - middle.astype(F32)).astype(BF16)


def dot_3(a, b):
    ah, am, al = split_3(a)
    bh, bm, bl = split_3(b)
    return lax.dot_general(
        jnp.concatenate([ah, ah, am, ah, am, al], axis=0),
        jnp.concatenate([bh, bm, bh, bl, bm, bh], axis=0),
        TN,
        preferred_element_type=F32,
    )


def fold(value, count):
    total = value[:B]
    for k in range(1, count):
        total = total + value[k * B : (k + 1) * B]
    return total


def room(mebibytes):
    return pltpu.CompilerParams(vmem_limit_bytes=mebibytes * 2**20)


def whole(shape):
    return pl.BlockSpec(shape, lambda i, *place: (0,) * len(shape))


def standardize(dosage, freq, individuals=1):
    allele = freq.astype(F32) / 10000.0
    spread = jnp.sqrt(2.0 * allele * (1.0 - allele))
    allele, spread = (jnp.expand_dims(value, individuals) for value in (allele, spread))
    scaled = (dosage.astype(F32) / 100.0 - 2.0 * allele) / spread
    return scaled.astype(BF16)


def strip_kernel(place_ref, source_ref, strip_ref, turned_ref):
    turned_ref[...] = source_ref[...].astype(F32).T
    strip_ref[...] = turned_ref[pl.ds(pl.multiple_of(place_ref[1], B), B), :]


def take_strip(source, offset):
    rows = source.shape[0]
    width = min(128, source.shape[1])
    place = jnp.stack([offset // width, offset % width]).astype(jnp.int32)
    return pl.pallas_call(
        strip_kernel,
        out_shape=jax.ShapeDtypeStruct((B, rows), F32),
        grid_spec=pltpu.PrefetchScalarGridSpec(
            num_scalar_prefetch=1,
            grid=(1,),
            in_specs=[pl.BlockSpec((rows, width), lambda i, place: (0, place[0]))],
            out_specs=pl.BlockSpec((B, rows), lambda i, place: (0, 0)),
            scratch_shapes=[pltpu.VMEM((width, rows), F32)],
        ),
        compiler_params=room(40),
        name="strip",
    )(place, source)


def hold_kernel(source_ref, held_ref, sem):
    copy = pltpu.make_async_copy(source_ref, held_ref, sem)
    copy.start()
    copy.wait()


def hold(source):
    held = pl.pallas_call(
        hold_kernel,
        out_shape=pltpu.VMEM(source.shape, source.dtype),
        in_specs=[pl.BlockSpec(memory_space=pltpu.HBM)],
        out_specs=pl.BlockSpec(memory_space=pltpu.VMEM),
        scratch_shapes=[pltpu.SemaphoreType.DMA],
        cost_estimate=pl.CostEstimate(
            flops=0, bytes_accessed=2 * source.size * 4, transcendentals=0
        ),
        compiler_params=room(16),
        name="hold",
    )(source)
    return pltpu.with_memory_space_constraint(held, pltpu.VMEM)


def grow_kernel(turned_ref, scaled_ref, relation_ref, grown_ref):
    step = relation_ref.shape[0]
    here = pl.ds(pl.multiple_of(pl.program_id(0) * step, step), step)
    grown_ref[here, :] = relation_ref[...] + jnp.dot(
        turned_ref[...], scaled_ref[...], preferred_element_type=F32
    )


def grow(turned, scaled, relation):
    rows, width = relation.shape
    step = min(256, rows)
    grown = pl.pallas_call(
        grow_kernel,
        out_shape=pltpu.VMEM((rows, width), F32),
        grid=(rows // step,),
        in_specs=[
            pl.BlockSpec((step, M), lambda i: (i, 0)),
            pl.BlockSpec((M, width), lambda i: (0, 0), pipeline_mode=pl.Buffered(1)),
            pl.BlockSpec((step, width), lambda i: (i, 0)),
        ],
        out_specs=pl.BlockSpec(memory_space=pltpu.VMEM),
        cost_estimate=pl.CostEstimate(
            flops=2 * M * rows * width, bytes_accessed=8 * rows * width, transcendentals=0
        ),
        compiler_params=room(20),
        name="grow",
    )(turned, scaled, relation)
    return pltpu.with_memory_space_constraint(grown, pltpu.VMEM)


def lifted(strip, ids, factor, lift):
    slots = lax.broadcasted_iota(jnp.int32, (B, 1), 0)
    select = jnp.where(ids == slots, 1.0, 0.0).astype(BF16)
    taken = lax.dot_general(
        jnp.concatenate(split_3(factor), axis=0),
        jnp.concatenate([select] * 3, axis=0),
        TN,
        preferred_element_type=F32,
    )
    return dot_3(lift, jnp.where(ids >= 0, strip, 0.0) - taken)


def lane_ids(width, start):
    return start + lax.broadcasted_iota(jnp.int32, (1, width), 1)


def panel_kernel(place_ref, raw_ref, chosen_ref, scaled_ref, strip_ref, small_ref):
    strip = raw_ref[...] + jnp.dot(
        chosen_ref[...], scaled_ref[...], preferred_element_type=F32
    ) * (1.0 / M)
    strip_ref[...] = strip
    ids = lane_ids(strip.shape[1], place_ref[0])
    slots = lax.broadcasted_iota(jnp.int32, (B, 1), 0)
    select = jnp.where(ids == slots, 1.0, 0.0).astype(BF16)
    parts = jnp.concatenate(split_3(strip), axis=0)
    rest = jnp.where(ids >= B, parts, jnp.zeros_like(parts))
    square = lax.dot_general(
        jnp.concatenate([select, rest], axis=0), parts, NT, preferred_element_type=F32
    )
    square = square[:, :B] + square[:, B : 2 * B] + square[:, 2 * B :]
    small_ref[:B, :] = square[:B]
    small_ref[B:, :] = fold(square[B:], 3)


def panel_block(place, raw, chosen, scaled):
    width = raw.shape[1]
    return pl.pallas_call(
        panel_kernel,
        out_shape=(
            jax.ShapeDtypeStruct((B, width), F32),
            jax.ShapeDtypeStruct((2 * B, B), F32),
        ),
        grid_spec=pltpu.PrefetchScalarGridSpec(
            num_scalar_prefetch=1,
            grid=(1,),
            in_specs=[whole(raw.shape), whole(chosen.shape), whole(scaled.shape)],
            out_specs=(whole((B, width)), whole((2 * B, B))),
        ),
        compiler_params=room(8),
        name="panel",
    )(place, raw, chosen, scaled)


def product_kernel(
    place_ref, strip_ref, factor_ref, lift_ref, scaled_ref, relation_ref,
    vecs_ref, sums_ref, marks_ref, columns_ref,
):
    @pl.when(pl.program_id(0) == 0)
    def _():
        width = strip_ref.shape[1]
        ids = lane_ids(width, place_ref[0])
        vecs = lifted(strip_ref[...], ids, factor_ref[...], lift_ref[...])
        vecs_ref[...] = vecs
        high, low = split(vecs)
        both = jnp.concatenate([high, low], axis=0)
        both = jnp.concatenate([both, jnp.zeros_like(both)], axis=0)
        columns_ref[...] = both.astype(F32).T.astype(BF16)
        marks_ref[...] = fold(
            lax.dot_general(both, scaled_ref[...], NT, preferred_element_type=F32), 2
        )

    step = sums_ref.shape[1]
    here = pl.ds(pl.multiple_of(pl.program_id(0) * step, step), step)
    high, low = split(relation_ref[here, :])
    columns = columns_ref[...]
    product = jnp.dot(high, columns, preferred_element_type=F32) + jnp.dot(
        low, columns, preferred_element_type=F32
    )
    sums_ref[...] = fold(product.T, 2)


def tile_product(place, strip, factor, lift, scaled, relation):
    rows, width = relation.shape
    step = min(256, rows)
    return pl.pallas_call(
        product_kernel,
        out_shape=(
            jax.ShapeDtypeStruct((B, width), F32),
            jax.ShapeDtypeStruct((B, rows), F32),
            jax.ShapeDtypeStruct((B, M), F32),
        ),
        grid_spec=pltpu.PrefetchScalarGridSpec(
            num_scalar_prefetch=1,
            grid=(rows // step,),
            in_specs=[
                whole(strip.shape),
                whole((B, B)),
                whole((B, B)),
                whole(scaled.shape),
                pl.BlockSpec(memory_space=pltpu.VMEM),
            ],
            out_specs=(
                whole((B, width)),
                pl.BlockSpec((B, step), lambda i, place: (0, i)),
                whole((B, M)),
            ),
            scratch_shapes=[pltpu.VMEM((width, 4 * B), BF16)],
        ),
        cost_estimate=pl.CostEstimate(
            flops=16 * B * rows * width, bytes_accessed=4 * rows * width, transcendentals=0
        ),
        compiler_params=room(16),
        name="product",
    )(place, strip, factor, lift, scaled, relation)


def rows_kernel(
    place_ref, raw_ref, chosen_ref, mine_ref, other_ref, factor_ref, lift_ref, sums_ref,
    vecs_ref, inner_ref, turned_ref,
):
    even = place_ref[1] == 0
    mine, other = mine_ref[...], other_ref[...]
    first = jnp.where(even, mine, other)
    second = jnp.where(even, other, mine)
    half = M // 2
    grown = jnp.dot(
        chosen_ref[:, :half], first, preferred_element_type=F32
    ) + jnp.dot(chosen_ref[:, half:], second, preferred_element_type=F32)
    strip = raw_ref[...] + grown * (1.0 / M)
    ids = lane_ids(strip.shape[1], place_ref[0])
    vecs = lifted(strip, ids, factor_ref[...], lift_ref[...])
    vecs_ref[...] = vecs
    square = lax.dot_general(
        jnp.concatenate(split(vecs), axis=0),
        jnp.concatenate(split(sums_ref[...]), axis=0),
        NT,
        preferred_element_type=F32,
    )
    inner_ref[...] = fold(square[:, :B] + square[:, B:], 2)
    turned_ref[:, :half] = (first.astype(F32) * (1.0 / M)).T.astype(BF16)
    turned_ref[:, half:] = (second.astype(F32) * (1.0 / M)).T.astype(BF16)


def row_block(place, raw, chosen, mine, other, factor, lift, sums):
    args = (raw, chosen, mine, other, factor, lift, sums)
    outs = ((raw.shape, F32), ((B, B), F32), ((raw.shape[1], M), BF16))
    return pl.pallas_call(
        rows_kernel,
        out_shape=tuple(jax.ShapeDtypeStruct(*out) for out in outs),
        grid_spec=pltpu.PrefetchScalarGridSpec(
            num_scalar_prefetch=1,
            grid=(1,),
            in_specs=[whole(a.shape) for a in args],
            out_specs=tuple(whole(out[0]) for out in outs),
        ),
        compiler_params=room(14),
        name="rows",
    )(place, *args)


def reflect_kernel(small_ref, factor_ref, lift_ref, triangle_ref):
    rows = lax.broadcasted_iota(jnp.int32, (B, B), 0)
    lanes = lax.broadcasted_iota(jnp.int32, (B, B), 1)
    row = lax.broadcasted_iota(jnp.int32, (B, 1), 0)
    lane = lax.broadcasted_iota(jnp.int32, (1, B), 1)
    eye = jnp.where(rows == lanes, 1.0, 0.0).astype(F32)
    work = small_ref[:B, :]
    cross = small_ref[B:, :]
    lift = eye
    triangle = jnp.zeros((B, B), F32)
    diagonal = jnp.zeros((1, B), F32)
    for j in range(B):
        column = jnp.where(row >= j, work[:, j : j + 1], 0.0)
        lift_column = lift[:, j : j + 1]
        cross_column = cross[:, j : j + 1]
        inner = jnp.sum(column * work, axis=0, keepdims=True) + jnp.sum(
            lift_column * cross, axis=0, keepdims=True
        )
        square = inner[:, j : j + 1]
        alpha = work[j : j + 1, j : j + 1]
        length = jnp.sqrt(square)
        shift = jnp.where(alpha >= 0.0, length, -length)
        tau = 1.0 / (length * (length + jnp.abs(alpha)))
        inner = inner + shift * work[j : j + 1, :]
        vector = column + jnp.where(row == j, shift, 0.0)
        kappa = jnp.where(lane > j, tau * inner, 0.0)
        work = work - vector * kappa
        work = work + jnp.where((rows == j) & (lanes == j), shift, 0.0)
        lift = lift - lift_column * kappa
        cross = cross - cross_column * kappa
        past = jnp.sum(triangle * jnp.where(lane < j, inner, 0.0), axis=1, keepdims=True)
        new = tau * (jnp.where(row == j, 1.0, 0.0) - past)
        triangle = jnp.where(lanes == j, new, triangle)
        diagonal = jnp.where(lane == j, -shift, diagonal)
    factor_ref[...] = jnp.where(rows < lanes, work, 0.0) + jnp.where(rows == lanes, diagonal, 0.0)
    lift_ref[...] = lift
    triangle_ref[...] = triangle


def reflect(small):
    out = jax.ShapeDtypeStruct((B, B), F32)
    return pl.pallas_call(
        reflect_kernel, out_shape=(out,) * 3, compiler_params=room(2), name="reflect"
    )(small)


def update_kernel(
    triangle_ref, inner_ref, marks_ref, turned_ref, vecs_rows_ref, sums_rows_ref,
    scaled_cols_ref, vecs_cols_ref, sums_cols_ref, relation_ref,
    out_ref, left_ref, half_ref,
):
    def dot(a, b, dims):
        return lax.dot_general(a, b, dims, precision=HIGH, preferred_element_type=F32)

    def parts(vecs, sums, scaled, dims, scale):
        marks = jnp.concatenate(split(marks_ref[...] * scale), axis=0)
        full = sums + fold(
            lax.dot_general(marks, scaled, dims, preferred_element_type=F32), 2
        )
        th, tl = split(triangle_ref[...])
        hh, hl = split(-half_ref[...])
        fh, fl = split(full)
        vh, vl = split(vecs)
        adjusted = lax.dot_general(
            jnp.concatenate([th, th, tl, hh, hh, hl], axis=0),
            jnp.concatenate([fh, fl, fh, vh, vl, vh], axis=0),
            TN,
            preferred_element_type=F32,
        )
        return (vh, vl) + split(adjusted)

    @pl.when(pl.program_id(0) == 0)
    def _():
        triangle = triangle_ref[...]
        marks = marks_ref[...]
        inner = inner_ref[...] + dot(marks, marks, NT) * (1.0 / M)
        half_ref[...] = 0.5 * dot(triangle, dot(inner, triangle, NN), TN)
        vh, vl, ah, al = parts(
            vecs_rows_ref[...], sums_rows_ref[...], turned_ref[...], NT, 1.0
        )
        left = jnp.concatenate([vh, vh, vl, vl, ah, ah, al, al], axis=0)
        left_ref[...] = left.astype(F32).T.astype(BF16)

    scaled = scaled_cols_ref[...]
    vh, vl, ah, al = parts(
        vecs_cols_ref[...], sums_cols_ref[...], scaled, NN, 1.0 / M
    )
    right = -jnp.concatenate([ah, al, ah, al, vh, vl, vh, vl], axis=0)
    rows, step = out_ref.shape
    here = pl.ds(pl.multiple_of(pl.program_id(0) * step, step), step)
    chunk = min(512, rows)
    for k in range(rows // chunk):
        some = pl.ds(k * chunk, chunk)
        out_ref[some, :] = (
            relation_ref[some, here]
            + jnp.dot(left_ref[some, :], right, preferred_element_type=F32)
        )


def tile_update(triangle, inner, marks, of_rows, of_cols, relation):
    rows, width = relation.shape
    step = min(512, width)

    def full(value):
        return pl.BlockSpec(value.shape, lambda i: (0, 0), pipeline_mode=pl.Buffered(1))

    def slab(value):
        return pl.BlockSpec((value.shape[0], step), lambda i: (0, i))

    fixed = (triangle, inner, marks) + of_rows
    return pl.pallas_call(
        update_kernel,
        out_shape=jax.ShapeDtypeStruct((rows, width), F32),
        grid=(width // step,),
        in_specs=[full(value) for value in fixed]
        + [slab(value) for value in of_cols]
        + [pl.BlockSpec(memory_space=pltpu.VMEM)],
        out_specs=slab(relation),
        scratch_shapes=[pltpu.VMEM((rows, 8 * B), BF16), pltpu.VMEM((B, B), F32)],
        cost_estimate=pl.CostEstimate(
            flops=16 * B * rows * width,
            bytes_accessed=4 * rows * width,
            transcendentals=0,
        ),
        compiler_params=room(20),
        name="update",
    )(*fixed, *of_cols, relation)


def swap(value, axis, size, bit):
    return lax.ppermute(value, axis, [(i, i ^ bit) for i in range(size)])


def bits_of(size):
    return [1 << b for b in range(size.bit_length() - 1)]


def make_body(n_row, n_col):
    per = n_row // n_col
    both = ("row", "col")

    def body(relation, dosage, freq, panel):
        tile_rows, tile_cols = relation.shape
        row_id = lax.axis_index("row")
        col_id = lax.axis_index("col")
        place = panel[0]
        first_row = (place + 1) * B
        panel_col = place * B // tile_cols
        panel_off = place * B % tile_cols
        own_col = row_id // per
        mine = row_id % per

        raw_rows = take_strip(relation, panel_off)
        apart = col_id ^ own_col
        place_cols = jnp.reshape(col_id * tile_cols - first_row, (1,)).astype(jnp.int32)
        place_rows = jnp.stack([row_id * tile_rows - first_row, col_id % 2]).astype(jnp.int32)
        even = col_id % 2 == 0
        at_own = own_col == col_id
        is_mine = [mine == s for s in range(per)]
        from_bit = [((col_id ^ panel_col) & bit) != 0 for bit in bits_of(n_col)]
        take_bit = [(apart & bit) != 0 for bit in bits_of(n_col)]
        shifts = [[(mine ^ s) == shift for shift in range(per)] for s in range(per)]
        scalars = (place_cols, place_rows, even, at_own, is_mine, from_bit, take_bit, shifts)
        ready, scalars = lax.optimization_barrier((relation, scalars))
        place_cols, place_rows, even, at_own, is_mine, from_bit, take_bit, shifts = scalars

        def from_panel(value, first, last):
            for k in range(first, last):
                other = swap(value, "col", n_col, 1 << k)
                value = jnp.where(from_bit[k], other, value)
            return value

        def halves(value, axis):
            size = value.shape[axis] // 2
            one = lax.slice_in_dim(value, 0, size, axis=axis)
            two = lax.slice_in_dim(value, size, 2 * size, axis=axis)
            return jnp.where(even, one, two), jnp.where(even, two, one)

        def rejoin(value, axis):
            other = swap(value, "col", n_col, 1)
            return jnp.concatenate(
                [jnp.where(even, value, other), jnp.where(even, other, value)], axis=axis
            )

        def to_column(block):
            total = jnp.where(at_own, block, 0.0)
            received = []
            for shift in range(1, n_col):
                pairs = []
                for c in range(n_col):
                    for s in range(per):
                        source = (c * per + s) * n_col + c
                        target = (((c + shift) % n_col) * per + s) * n_col + c
                        pairs.append((source, target))
                received.append(lax.ppermute(block, both, pairs))
            for other in received:
                total = total + other
            return total

        def join_column(block):
            parts = [None] * per
            got = [block]
            for shift in range(1, per):
                pairs = [
                    (r, (r // per) * per + (r % per) ^ shift) for r in range(n_row)
                ]
                got.append(lax.ppermute(block, "row", pairs))
            for s in range(per):
                value = got[0]
                for shift in range(1, per):
                    value = jnp.where(shifts[s][shift], got[shift], value)
                parts[s] = value
            return jnp.concatenate(parts, axis=1)

        log_col = n_col.bit_length() - 1
        raw_rows = from_panel(raw_rows, 0, 1)
        dosage, raw_rows = lax.optimization_barrier((dosage, raw_rows))
        scaled = standardize(dosage, freq)
        chosen = take_strip(dosage, panel_off)
        chosen = from_panel(standardize(chosen, freq, 0), 0, log_col)
        raw_rows = from_panel(raw_rows, 1, log_col)

        own = scaled[:, :tile_rows]
        for k in range(1, per):
            own = jnp.where(is_mine[k], scaled[:, k * tile_rows : (k + 1) * tile_rows], own)

        def spread_rows(value, bit):
            pairs = []
            for r in range(n_row):
                for c in range(n_col):
                    apart = c ^ (r // per)
                    if bit == 1:
                        if apart == 0:
                            pairs.append((r * n_col + c, r * n_col + (c ^ 1)))
                    elif (apart & ~1) & ~(bit - 1) == 0:
                        pairs.append((r * n_col + c, r * n_col + (c ^ bit)))
            other = lax.ppermute(value, both, pairs)
            return jnp.where(take_bit[bit.bit_length() - 1], other, value)

        own = spread_rows(own, 1)
        part, _ = halves(own, 0)
        part, raw_rows, ready = lax.optimization_barrier((part, raw_rows, ready))
        for bit in bits_of(n_col)[1:]:
            part = spread_rows(part, bit)
        other_part = swap(part, "col", n_col, 1)

        raw_cols, held = lax.optimization_barrier((to_column(raw_rows), hold(ready)))
        raw_cols = join_column(raw_cols)
        strip_cols, small = panel_block(place_cols, raw_cols, chosen, scaled)
        for bit in bits_of(n_col):
            small = small + swap(small, "col", n_col, bit)
        small, other_part = lax.optimization_barrier((small, other_part))
        factor, lift, triangle = reflect(small)

        vecs_cols, part_sums, part_marks = tile_product(
            place_cols, strip_cols, factor, lift, scaled, held
        )
        vecs_rows, inner, turned = row_block(
            place_rows, raw_rows, chosen, part, other_part, factor, lift, part_sums
        )
        kept, sent = halves(jnp.concatenate([part_sums, part_marks], axis=1), 1)
        kept = jnp.concatenate([kept, inner], axis=1)
        sent = jnp.concatenate([sent, inner], axis=1)
        kept = kept + swap(sent, "col", n_col, 1)
        for bit in bits_of(n_col)[1:]:
            kept = kept + swap(kept, "col", n_col, bit)
        inner = kept[:, -B:]
        sums = rejoin(kept[:, :-B], 1)
        sums_rows, marks = sums[:, :tile_rows], sums[:, tile_rows:]

        near = inner
        for shift in range(1, per):
            pairs = [(r, (r // per) * per + (r % per) ^ shift) for r in range(n_row)]
            near = near + lax.ppermute(inner, "row", pairs)
        sums_rows, ready, turned = lax.optimization_barrier((sums_rows, ready, turned))
        ready, near = lax.optimization_barrier((ready, near))
        sums_cols, held, near = lax.optimization_barrier(
            (to_column(sums_rows), grow(turned, scaled, ready), near)
        )
        inner = near
        for shift in range(1, n_col):
            pairs = [(r, (r + shift * per) % n_row) for r in range(n_row)]
            inner = inner + lax.ppermute(near, "row", pairs)
        sums_cols = join_column(sums_cols)
        return tile_update(
            triangle,
            inner,
            marks,
            (turned, vecs_rows, sums_rows),
            (scaled, vecs_cols, sums_cols),
            held,
        )

    return body


def solution(mesh):
    placed = (P("row", "col"), P(None, "col"), P(), P())
    body = make_body(mesh.shape["row"], mesh.shape["col"])
    return jax.shard_map(
        body, mesh=mesh, in_specs=placed, out_specs=P("row", "col"), check_vma=False
    )
```

```python
import jax
import jax.numpy as jnp
from jax import lax
from jax.experimental import pallas as pl
from jax.experimental.pallas import tpu as pltpu
from jax.sharding import PartitionSpec as P


B = 32
M = 512
F32 = jnp.float32
BF16 = jnp.bfloat16
HIGH = lax.Precision.HIGHEST
NN = (((1,), (0,)), ((), ()))
NT = (((1,), (1,)), ((), ()))
TN = (((0,), (0,)), ((), ()))


def split(value):
    high = value.astype(BF16)
    return high, (value - high.astype(F32)).astype(BF16)


def split_3(value):
    high = value.astype(BF16)
    rest = value - high.astype(F32)
    middle = rest.astype(BF16)
    return high, middle, (rest - middle.astype(F32)).astype(BF16)


def dot_3(a, b):
    ah, am, al = split_3(a)
    bh, bm, bl = split_3(b)
    return lax.dot_general(
        jnp.concatenate([ah, ah, am, ah, am, al], axis=0),
        jnp.concatenate([bh, bm, bh, bl, bm, bh], axis=0),
        TN,
        preferred_element_type=F32,
    )


def fold(value, count):
    total = value[:B]
    for k in range(1, count):
        total = total + value[k * B : (k + 1) * B]
    return total


def room(mebibytes):
    return pltpu.CompilerParams(vmem_limit_bytes=mebibytes * 2**20)


def whole(shape):
    return pl.BlockSpec(shape, lambda i, *place: (0,) * len(shape))


def standardize(dosage, freq, individuals=1):
    allele = freq.astype(F32) / 10000.0
    spread = jnp.sqrt(2.0 * allele * (1.0 - allele))
    allele, spread = (jnp.expand_dims(value, individuals) for value in (allele, spread))
    scaled = (dosage.astype(F32) / 100.0 - 2.0 * allele) / spread
    return scaled.astype(BF16)


def strip_kernel(place_ref, source_ref, strip_ref, turned_ref):
    turned_ref[...] = source_ref[...].astype(F32).T
    strip_ref[...] = turned_ref[pl.ds(pl.multiple_of(place_ref[1], B), B), :]


def take_strip(source, offset):
    rows = source.shape[0]
    width = min(128, source.shape[1])
    place = jnp.stack([offset // width, offset % width]).astype(jnp.int32)
    return pl.pallas_call(
        strip_kernel,
        out_shape=jax.ShapeDtypeStruct((B, rows), F32),
        grid_spec=pltpu.PrefetchScalarGridSpec(
            num_scalar_prefetch=1,
            grid=(1,),
            in_specs=[pl.BlockSpec((rows, width), lambda i, place: (0, place[0]))],
            out_specs=pl.BlockSpec((B, rows), lambda i, place: (0, 0)),
            scratch_shapes=[pltpu.VMEM((width, rows), F32)],
        ),
        compiler_params=room(58),
        name="strip",
    )(place, source)


def hold_kernel(source_ref, held_ref, sem):
    copy = pltpu.make_async_copy(source_ref, held_ref, sem)
    copy.start()
    copy.wait()


def hold(source):
    held = pl.pallas_call(
        hold_kernel,
        out_shape=pltpu.VMEM(source.shape, source.dtype),
        in_specs=[pl.BlockSpec(memory_space=pltpu.HBM)],
        out_specs=pl.BlockSpec(memory_space=pltpu.VMEM),
        scratch_shapes=[pltpu.SemaphoreType.DMA],
        cost_estimate=pl.CostEstimate(
            flops=0, bytes_accessed=2 * source.size * 4, transcendentals=0
        ),
        compiler_params=room(16),
        name="hold",
    )(source)
    return pltpu.with_memory_space_constraint(held, pltpu.VMEM)


def grow_kernel(turned_ref, scaled_ref, relation_ref, grown_ref):
    rows, step = relation_ref.shape
    here = pl.ds(pl.multiple_of(pl.program_id(0) * step, step), step)
    chunk = min(512, rows)
    for k in range(rows // chunk):
        some = pl.ds(k * chunk, chunk)
        grown_ref[some, here] = relation_ref[some, :] + jnp.dot(
            turned_ref[some, :], scaled_ref[...], preferred_element_type=F32
        )


def grow(turned, scaled, relation):
    rows, width = relation.shape
    step = min(512, width)
    grown = pl.pallas_call(
        grow_kernel,
        out_shape=pltpu.VMEM((rows, width), F32),
        grid=(width // step,),
        in_specs=[
            pl.BlockSpec((rows, M), lambda i: (0, 0), pipeline_mode=pl.Buffered(1)),
            pl.BlockSpec((M, step), lambda i: (0, i)),
            pl.BlockSpec((rows, step), lambda i: (0, i)),
        ],
        out_specs=pl.BlockSpec(memory_space=pltpu.VMEM),
        cost_estimate=pl.CostEstimate(
            flops=2 * M * rows * width, bytes_accessed=8 * rows * width, transcendentals=0
        ),
        compiler_params=room(20),
        name="grow",
    )(turned, scaled, relation)
    return pltpu.with_memory_space_constraint(grown, pltpu.VMEM)


def lifted(strip, ids, factor, lift):
    slots = lax.broadcasted_iota(jnp.int32, (B, 1), 0)
    select = jnp.where(ids == slots, 1.0, 0.0).astype(BF16)
    taken = lax.dot_general(
        jnp.concatenate(split_3(factor), axis=0),
        jnp.concatenate([select] * 3, axis=0),
        TN,
        preferred_element_type=F32,
    )
    return dot_3(lift, jnp.where(ids >= 0, strip, 0.0) - taken)


def lane_ids(width, start):
    return start + lax.broadcasted_iota(jnp.int32, (1, width), 1)


def panel_kernel(place_ref, raw_ref, chosen_ref, scaled_ref, strip_ref, small_ref):
    strip = raw_ref[...] + jnp.dot(
        chosen_ref[...], scaled_ref[...], preferred_element_type=F32
    ) * (1.0 / M)
    strip_ref[...] = strip
    ids = lane_ids(strip.shape[1], place_ref[0])
    slots = lax.broadcasted_iota(jnp.int32, (B, 1), 0)
    select = jnp.where(ids == slots, 1.0, 0.0).astype(BF16)
    parts = jnp.concatenate(split_3(strip), axis=0)
    rest = jnp.where(ids >= B, parts, jnp.zeros_like(parts))
    square = lax.dot_general(
        jnp.concatenate([select, rest], axis=0), parts, NT, preferred_element_type=F32
    )
    square = square[:, :B] + square[:, B : 2 * B] + square[:, 2 * B :]
    small_ref[:B, :] = square[:B]
    small_ref[B:, :] = fold(square[B:], 3)


def panel_block(place, raw, chosen, scaled):
    width = raw.shape[1]
    return pl.pallas_call(
        panel_kernel,
        out_shape=(
            jax.ShapeDtypeStruct((B, width), F32),
            jax.ShapeDtypeStruct((2 * B, B), F32),
        ),
        grid_spec=pltpu.PrefetchScalarGridSpec(
            num_scalar_prefetch=1,
            grid=(1,),
            in_specs=[whole(raw.shape), whole(chosen.shape), whole(scaled.shape)],
            out_specs=(whole((B, width)), whole((2 * B, B))),
        ),
        compiler_params=room(8),
        name="panel",
    )(place, raw, chosen, scaled)


def product_kernel(
    place_ref, strip_ref, factor_ref, lift_ref, scaled_ref, relation_ref,
    vecs_ref, sums_ref, marks_ref, columns_ref,
):
    @pl.when(pl.program_id(0) == 0)
    def _():
        width = strip_ref.shape[1]
        ids = lane_ids(width, place_ref[0])
        vecs = lifted(strip_ref[...], ids, factor_ref[...], lift_ref[...])
        vecs_ref[...] = vecs
        high, low = split(vecs)
        both = jnp.concatenate([high, low], axis=0)
        both = jnp.concatenate([both, jnp.zeros_like(both)], axis=0)
        columns_ref[...] = both.astype(F32).T.astype(BF16)
        marks_ref[...] = fold(
            lax.dot_general(both, scaled_ref[...], NT, preferred_element_type=F32), 2
        )

    step = sums_ref.shape[1]
    here = pl.ds(pl.multiple_of(pl.program_id(0) * step, step), step)
    high, low = split(relation_ref[here, :])
    columns = columns_ref[...]
    product = jnp.dot(high, columns, preferred_element_type=F32) + jnp.dot(
        low, columns, preferred_element_type=F32
    )
    sums_ref[...] = fold(product.T, 2)


def tile_product(place, strip, factor, lift, scaled, relation):
    rows, width = relation.shape
    step = min(256, rows)
    return pl.pallas_call(
        product_kernel,
        out_shape=(
            jax.ShapeDtypeStruct((B, width), F32),
            jax.ShapeDtypeStruct((B, rows), F32),
            jax.ShapeDtypeStruct((B, M), F32),
        ),
        grid_spec=pltpu.PrefetchScalarGridSpec(
            num_scalar_prefetch=1,
            grid=(rows // step,),
            in_specs=[
                whole(strip.shape),
                whole((B, B)),
                whole((B, B)),
                whole(scaled.shape),
                pl.BlockSpec(memory_space=pltpu.VMEM),
            ],
            out_specs=(
                whole((B, width)),
                pl.BlockSpec((B, step), lambda i, place: (0, i)),
                whole((B, M)),
            ),
            scratch_shapes=[pltpu.VMEM((width, 4 * B), BF16)],
        ),
        cost_estimate=pl.CostEstimate(
            flops=16 * B * rows * width, bytes_accessed=4 * rows * width, transcendentals=0
        ),
        compiler_params=room(16),
        name="product",
    )(place, strip, factor, lift, scaled, relation)


def rows_kernel(
    place_ref, raw_ref, chosen_ref, mine_ref, other_ref, factor_ref, lift_ref, sums_ref,
    vecs_ref, inner_ref, turned_ref,
):
    even = place_ref[1] == 0
    mine, other = mine_ref[...], other_ref[...]
    first = jnp.where(even, mine, other)
    second = jnp.where(even, other, mine)
    half = M // 2
    grown = jnp.dot(
        chosen_ref[:, :half], first, preferred_element_type=F32
    ) + jnp.dot(chosen_ref[:, half:], second, preferred_element_type=F32)
    strip = raw_ref[...] + grown * (1.0 / M)
    ids = lane_ids(strip.shape[1], place_ref[0])
    vecs = lifted(strip, ids, factor_ref[...], lift_ref[...])
    vecs_ref[...] = vecs
    square = lax.dot_general(
        jnp.concatenate(split(vecs), axis=0),
        jnp.concatenate(split(sums_ref[...]), axis=0),
        NT,
        preferred_element_type=F32,
    )
    inner_ref[...] = fold(square[:, :B] + square[:, B:], 2)
    turned_ref[:, :half] = (first.astype(F32) * (1.0 / M)).T.astype(BF16)
    turned_ref[:, half:] = (second.astype(F32) * (1.0 / M)).T.astype(BF16)


def row_block(place, raw, chosen, mine, other, factor, lift, sums):
    args = (raw, chosen, mine, other, factor, lift, sums)
    outs = ((raw.shape, F32), ((B, B), F32), ((raw.shape[1], M), BF16))
    return pl.pallas_call(
        rows_kernel,
        out_shape=tuple(jax.ShapeDtypeStruct(*out) for out in outs),
        grid_spec=pltpu.PrefetchScalarGridSpec(
            num_scalar_prefetch=1,
            grid=(1,),
            in_specs=[whole(a.shape) for a in args],
            out_specs=tuple(whole(out[0]) for out in outs),
        ),
        compiler_params=room(14),
        name="rows",
    )(place, *args)


def reflect_kernel(small_ref, factor_ref, lift_ref, triangle_ref):
    rows = lax.broadcasted_iota(jnp.int32, (B, B), 0)
    lanes = lax.broadcasted_iota(jnp.int32, (B, B), 1)
    row = lax.broadcasted_iota(jnp.int32, (B, 1), 0)
    lane = lax.broadcasted_iota(jnp.int32, (1, B), 1)
    eye = jnp.where(rows == lanes, 1.0, 0.0).astype(F32)
    work = small_ref[:B, :]
    cross = small_ref[B:, :]
    lift = eye
    triangle = jnp.zeros((B, B), F32)
    diagonal = jnp.zeros((1, B), F32)
    for j in range(B):
        column = jnp.where(row >= j, work[:, j : j + 1], 0.0)
        lift_column = lift[:, j : j + 1]
        cross_column = cross[:, j : j + 1]
        inner = jnp.sum(column * work, axis=0, keepdims=True) + jnp.sum(
            lift_column * cross, axis=0, keepdims=True
        )
        square = inner[:, j : j + 1]
        alpha = work[j : j + 1, j : j + 1]
        length = jnp.sqrt(square)
        shift = jnp.where(alpha >= 0.0, length, -length)
        tau = 1.0 / (length * (length + jnp.abs(alpha)))
        inner = inner + shift * work[j : j + 1, :]
        vector = column + jnp.where(row == j, shift, 0.0)
        kappa = jnp.where(lane > j, tau * inner, 0.0)
        work = work - vector * kappa
        work = work + jnp.where((rows == j) & (lanes == j), shift, 0.0)
        lift = lift - lift_column * kappa
        cross = cross - cross_column * kappa
        past = jnp.sum(triangle * jnp.where(lane < j, inner, 0.0), axis=1, keepdims=True)
        new = tau * (jnp.where(row == j, 1.0, 0.0) - past)
        triangle = jnp.where(lanes == j, new, triangle)
        diagonal = jnp.where(lane == j, -shift, diagonal)
    factor_ref[...] = jnp.where(rows < lanes, work, 0.0) + jnp.where(rows == lanes, diagonal, 0.0)
    lift_ref[...] = lift
    triangle_ref[...] = triangle


def reflect(small):
    out = jax.ShapeDtypeStruct((B, B), F32)
    return pl.pallas_call(
        reflect_kernel, out_shape=(out,) * 3, compiler_params=room(2), name="reflect"
    )(small)


def update_kernel(
    triangle_ref, inner_ref, marks_ref, turned_ref, vecs_rows_ref, sums_rows_ref,
    scaled_cols_ref, vecs_cols_ref, sums_cols_ref, relation_ref,
    out_ref, left_ref, right_ref, half_ref,
):
    def dot(a, b, dims):
        return lax.dot_general(a, b, dims, precision=HIGH, preferred_element_type=F32)

    def parts(vecs, sums, scaled, dims, scale):
        marks = jnp.concatenate(split(marks_ref[...] * scale), axis=0)
        full = sums + fold(
            lax.dot_general(marks, scaled, dims, preferred_element_type=F32), 2
        )
        th, tl = split(triangle_ref[...])
        hh, hl = split(-half_ref[...])
        fh, fl = split(full)
        vh, vl = split(vecs)
        adjusted = lax.dot_general(
            jnp.concatenate([th, th, tl, hh, hh, hl], axis=0),
            jnp.concatenate([fh, fl, fh, vh, vl, vh], axis=0),
            TN,
            preferred_element_type=F32,
        )
        return (vh, vl) + split(adjusted)

    @pl.when(pl.program_id(0) == 0)
    def _():
        triangle = triangle_ref[...]
        marks = marks_ref[...]
        inner = inner_ref[...] + dot(marks, marks, NT) * (1.0 / M)
        half_ref[...] = 0.5 * dot(triangle, dot(inner, triangle, NN), TN)
        vh, vl, ah, al = parts(
            vecs_rows_ref[...], sums_rows_ref[...], turned_ref[...], NT, 1.0
        )
        left = jnp.concatenate([vh, vh, vl, vl, ah, ah, al, al], axis=0)
        left_ref[...] = left.astype(F32).T.astype(BF16)
        vh, vl, ah, al = parts(
            vecs_cols_ref[...], sums_cols_ref[...], scaled_cols_ref[...], NN, 1.0 / M
        )
        right_ref[...] = -jnp.concatenate([ah, al, ah, al, vh, vl, vh, vl], axis=0)

    rows, step = out_ref.shape
    here = pl.ds(pl.multiple_of(pl.program_id(0) * step, step), step)
    chunk = min(512, rows)
    for k in range(rows // chunk):
        some = pl.ds(k * chunk, chunk)
        out_ref[some, :] = (
            relation_ref[some, here]
            + jnp.dot(left_ref[some, :], right_ref[:, here], preferred_element_type=F32)
        )


def tile_update(triangle, inner, marks, of_rows, of_cols, relation):
    rows, width = relation.shape
    step = min(512, width)

    def full(value):
        return pl.BlockSpec(value.shape, lambda i: (0, 0), pipeline_mode=pl.Buffered(1))

    def slab(value):
        return pl.BlockSpec((value.shape[0], step), lambda i: (0, i))

    fixed = (triangle, inner, marks) + of_rows + of_cols
    return pl.pallas_call(
        update_kernel,
        out_shape=jax.ShapeDtypeStruct((rows, width), F32),
        grid=(width // step,),
        in_specs=[full(value) for value in fixed]
        + [pl.BlockSpec(memory_space=pltpu.VMEM)],
        out_specs=slab(relation),
        scratch_shapes=[
            pltpu.VMEM((rows, 8 * B), BF16),
            pltpu.VMEM((8 * B, width), BF16),
            pltpu.VMEM((B, B), F32),
        ],
        cost_estimate=pl.CostEstimate(
            flops=16 * B * rows * width,
            bytes_accessed=4 * rows * width,
            transcendentals=0,
        ),
        compiler_params=room(20),
        name="update",
    )(*fixed, relation)


def swap(value, axis, size, bit):
    return lax.ppermute(value, axis, [(i, i ^ bit) for i in range(size)])


def bits_of(size):
    return [1 << b for b in range(size.bit_length() - 1)]


def make_body(n_row, n_col):
    per = n_row // n_col
    both = ("row", "col")

    def body(relation, dosage, freq, panel):
        tile_rows, tile_cols = relation.shape
        row_id = lax.axis_index("row")
        col_id = lax.axis_index("col")
        place = panel[0]
        first_row = (place + 1) * B
        panel_col = place * B // tile_cols
        panel_off = place * B % tile_cols
        own_col = row_id // per
        mine = row_id % per

        raw_rows = take_strip(relation, panel_off)
        apart = col_id ^ own_col
        place_cols = jnp.reshape(col_id * tile_cols - first_row, (1,)).astype(jnp.int32)
        place_rows = jnp.stack([row_id * tile_rows - first_row, col_id % 2]).astype(jnp.int32)
        even = col_id % 2 == 0
        at_own = own_col == col_id
        is_mine = [mine == s for s in range(per)]
        from_bit = [((col_id ^ panel_col) & bit) != 0 for bit in bits_of(n_col)]
        take_bit = [(apart & bit) != 0 for bit in bits_of(n_col)]
        shifts = [[(mine ^ s) == shift for shift in range(per)] for s in range(per)]
        scalars = (place_cols, place_rows, even, at_own, is_mine, from_bit, take_bit, shifts)
        ready, scalars = lax.optimization_barrier((relation, scalars))
        place_cols, place_rows, even, at_own, is_mine, from_bit, take_bit, shifts = scalars

        def from_panel(value, first, last):
            for k in range(first, last):
                other = swap(value, "col", n_col, 1 << k)
                value = jnp.where(from_bit[k], other, value)
            return value

        def halves(value, axis):
            size = value.shape[axis] // 2
            one = lax.slice_in_dim(value, 0, size, axis=axis)
            two = lax.slice_in_dim(value, size, 2 * size, axis=axis)
            return jnp.where(even, one, two), jnp.where(even, two, one)

        def rejoin(value, axis):
            other = swap(value, "col", n_col, 1)
            return jnp.concatenate(
                [jnp.where(even, value, other), jnp.where(even, other, value)], axis=axis
            )

        def to_column(block):
            total = jnp.where(at_own, block, 0.0)
            received = []
            for shift in range(1, n_col):
                pairs = []
                for c in range(n_col):
                    for s in range(per):
                        source = (c * per + s) * n_col + c
                        target = (((c + shift) % n_col) * per + s) * n_col + c
                        pairs.append((source, target))
                received.append(lax.ppermute(block, both, pairs))
            for other in received:
                total = total + other
            return total

        def join_column(block):
            parts = [None] * per
            got = [block]
            for shift in range(1, per):
                pairs = [
                    (r, (r // per) * per + (r % per) ^ shift) for r in range(n_row)
                ]
                got.append(lax.ppermute(block, "row", pairs))
            for s in range(per):
                value = got[0]
                for shift in range(1, per):
                    value = jnp.where(shifts[s][shift], got[shift], value)
                parts[s] = value
            return jnp.concatenate(parts, axis=1)

        log_col = n_col.bit_length() - 1
        chosen = standardize(take_strip(dosage, panel_off), freq, 0)
        raw_rows, chosen = lax.optimization_barrier((raw_rows, chosen))
        raw_rows, chosen = from_panel(raw_rows, 0, 1), from_panel(chosen, 0, 1)
        dosage, raw_rows, chosen = lax.optimization_barrier((dosage, raw_rows, chosen))
        scaled = standardize(dosage, freq)
        raw_rows = from_panel(raw_rows, 1, log_col)
        chosen = from_panel(chosen, 1, log_col)

        own = scaled[:, :tile_rows]
        for k in range(1, per):
            own = jnp.where(is_mine[k], scaled[:, k * tile_rows : (k + 1) * tile_rows], own)

        def spread_rows(value, bit):
            pairs = []
            for r in range(n_row):
                for c in range(n_col):
                    apart = c ^ (r // per)
                    if bit == 1:
                        if apart == 0:
                            pairs.append((r * n_col + c, r * n_col + (c ^ 1)))
                    elif (apart & ~1) & ~(bit - 1) == 0:
                        pairs.append((r * n_col + c, r * n_col + (c ^ bit)))
            other = lax.ppermute(value, both, pairs)
            return jnp.where(take_bit[bit.bit_length() - 1], other, value)

        own = spread_rows(own, 1)
        part, _ = halves(own, 0)
        part, raw_rows, chosen, ready = lax.optimization_barrier(
            (part, raw_rows, chosen, ready)
        )
        for bit in bits_of(n_col)[1:]:
            part = spread_rows(part, bit)
        other_part = swap(part, "col", n_col, 1)

        raw_cols, held = lax.optimization_barrier((to_column(raw_rows), hold(ready)))
        raw_cols = join_column(raw_cols)
        strip_cols, small = panel_block(place_cols, raw_cols, chosen, scaled)
        for bit in bits_of(n_col):
            small = small + swap(small, "col", n_col, bit)
        small, other_part = lax.optimization_barrier((small, other_part))
        factor, lift, triangle = reflect(small)

        vecs_cols, part_sums, part_marks = tile_product(
            place_cols, strip_cols, factor, lift, scaled, held
        )
        vecs_rows, inner, turned = row_block(
            place_rows, raw_rows, chosen, part, other_part, factor, lift, part_sums
        )
        kept, sent = halves(jnp.concatenate([part_sums, part_marks], axis=1), 1)
        kept = jnp.concatenate([kept, inner], axis=1)
        sent = jnp.concatenate([sent, inner], axis=1)
        kept = kept + swap(sent, "col", n_col, 1)
        for bit in bits_of(n_col)[1:]:
            kept = kept + swap(kept, "col", n_col, bit)
        inner = kept[:, -B:]
        sums = rejoin(kept[:, :-B], 1)
        sums_rows, marks = sums[:, :tile_rows], sums[:, tile_rows:]

        near = inner
        for shift in range(1, per):
            pairs = [(r, (r // per) * per + (r % per) ^ shift) for r in range(n_row)]
            near = near + lax.ppermute(inner, "row", pairs)
        sums_rows, ready, turned = lax.optimization_barrier((sums_rows, ready, turned))
        held = grow(turned, scaled, ready)
        sums_cols, held = lax.optimization_barrier((to_column(sums_rows), held))
        inner = near
        for shift in range(1, n_col):
            pairs = [(r, (r + shift * per) % n_row) for r in range(n_row)]
            inner = inner + lax.ppermute(near, "row", pairs)
        sums_cols = join_column(sums_cols)
        return tile_update(
            triangle,
            inner,
            marks,
            (turned, vecs_rows, sums_rows),
            (scaled, vecs_cols, sums_cols),
            held,
        )

    return body


def solution(mesh):
    placed = (P("row", "col"), P(None, "col"), P(), P())
    body = make_body(mesh.shape["row"], mesh.shape["col"])
    return jax.shard_map(
        body, mesh=mesh, in_specs=placed, out_specs=P("row", "col"), check_vma=False
    )
```
